32 devices in a mesh: dp: 8 (over y, x, core), tensor: 4 (over z).
Axes of the slice: x: 2, y: 2, z: 4, core: 2. Of those that a mesh axis runs over, the one named last changes fastest.
Arguments:
- hidden_in: bfloat16 [2048, 8192], P('dp'), may hold values from -6 to 6
- queries: bfloat16 [2048, 8192], P('dp', 'tensor'), may hold values from -8 to 8
- keys: bfloat16 [2048, 1024], P('dp', 'tensor'), may hold values from -8 to 8
- value_weight: bfloat16 [8192, 1024], P('dp', 'tensor'), may hold values from -0.0625 to 0.0625
- context_grad: bfloat16 [2048, 8192], P('dp', 'tensor'), may hold values from -6 to 6
- doc_ids: int32 [8, 256], P('dp'), may hold values from 0 to 15, never falling along the last dimension, each value on 1 to 128 neighbouring positions
- token_counts: int32 [8], P('dp'), may hold values from 64 to 256, as said below
Outputs:
- context: bfloat16 [2048, 8192], P('dp', 'tensor')
- w_value_grad: float32 [8192, 1024], P('dp', 'tensor')
The draws below stay inside these ranges and needn't reach their ends.
Inputs may be any that keep to these rules, and one draw needn't show every extreme that they name: `token_counts`: every replica has at least 64 tokens with a loss, and some replica has all 256; its other rows are padding. `doc_ids`: within a replica documents are numbered in order; a document has 1 to 128 tokens.
All inputs are finite; a program needn't handle non-finite values.
Results may differ from the reference program's by a relative error of at most 0.0054.
Values may be sent and summed in bfloat16 or wider, within the bound.
A program may use at most 64 MiB of HBM per device.

```python
import math
import jax
import jax.numpy as jnp
import numpy as np
from jax import lax

MODEL_WIDTH = 8192
QUERY_HEADS = 64
KEY_VALUE_HEADS = 8
HEAD_SIZE = 128
REPLICA_TOKENS = 256
TOKENS = 2048
N_DP = 8


def unmasked_rows(key, cols):
    return jnp.clip(jax.random.normal(key, (TOKENS, cols), jnp.float32), -6.0, 6.0)


def draw_queries(key, part):
    base_offset = unmasked_rows(jax.random.fold_in(key, 21), QUERY_HEADS * HEAD_SIZE)
    return base_offset.astype(jnp.bfloat16)


def draw_keys(key, part):
    base_offset = unmasked_rows(jax.random.fold_in(key, 31), KEY_VALUE_HEADS * HEAD_SIZE)
    return base_offset.astype(jnp.bfloat16)


def draw_token_counts(key, part):
    replica = jnp.arange(N_DP, dtype=jnp.int32)
    base_offset = REPLICA_TOKENS // 4 + replica * (REPLICA_TOKENS // 2) // max(N_DP - 1, 1)
    extra = jax.random.randint(jax.random.fold_in(key, 41), (N_DP,), 0, REPLICA_TOKENS // 4 + 1)
    chosen = jax.random.randint(jax.random.fold_in(key, 43), (), 0, N_DP)
    counts = jnp.minimum(base_offset + extra, REPLICA_TOKENS)
    return jnp.where(replica == chosen, REPLICA_TOKENS, counts).astype(jnp.int32)


def with_spikes(drawn, own_key, source, target, parts, factor):
    owner, partner = [(jnp.arange(drawn.shape[dim]) // (drawn.shape[dim] // parts)).reshape([-1 if axis == dim else 1 for axis in range(drawn.ndim)]) for dim in (source, target)]
    chosen = jax.random.permutation(own_key, parts)[partner]
    strong = (owner == chosen) | (owner == (partner + parts // 2) % parts)
    return jnp.where(strong, factor * drawn, drawn)


def block_scale(stream_key, extent, shards, low, largest):
    def one(dim, blocks):
        heights = jax.random.uniform(jax.random.fold_in(jax.random.fold_in(stream_key, 6), dim), (blocks,), jnp.float32, low / len(shards), largest / len(shards))
        return jnp.repeat(jnp.exp(heights), extent[dim] // blocks).reshape((-1,) + (1,) * (len(extent) - dim - 1))

    level = one(*shards[0])
    for cut in shards[1:]:
        level = level * one(*cut)
    return level


def profile(count, total, limit, skew):
    portions = [(1 << 20) // math.isqrt(standing ** skew) + 1 for standing in range(2, count + 1)]
    spare, given = total - limit - (count - 1), [1] * (count - 1)
    while spare > 0:
        candidates = [i for i in range(count - 1) if given[i] < limit]
        whole, left = sum([portions[i] for i in candidates]), spare
        for i in candidates:
            addition = min(limit - given[i], max(1, left * portions[i] // whole), spare)
            given[i] = given[i] + addition
            spare = spare - addition
    return np.array([limit] + given)


def ragged(key, count, total, limit, slope):
    if count == 2:
        one = jax.random.randint(key, (), max(1, total - limit), min(limit, total - 1) + 1)
        return jnp.stack([one, total - one])
    tallies = jnp.asarray(profile(count, total, limit, slope), jnp.int32)
    couples = (count - 1) // 2
    giver, taker = tallies[1:1 + 2 * couples:2], tallies[2:2 + 2 * couples:2]
    slack = jnp.minimum(giver - 1, limit - taker)
    moved = jax.random.randint(jax.random.fold_in(key, 1), (couples,), 0, 1 << 20) % (slack + 1)
    tallies = tallies.at[1:1 + 2 * couples:2].set(giver - moved).at[2:2 + 2 * couples:2].set(taker + moved)
    return tallies[jax.random.permutation(jax.random.fold_in(key, 2), count)]


def centred(key, shape, scale, bound, pieces=(), kind=jnp.bfloat16):
    array = scale * jax.random.normal(key, shape, jnp.float32)
    if pieces:
        array = array * block_scale(key, shape, pieces, -0.22, 0.18)
    return jnp.clip(array, -bound, bound).astype(kind)


def heavy_noise(own_key, shape, deviation, bound, cuts, heavy, kind=jnp.bfloat16):
    result = deviation * jax.random.normal(own_key, shape, jnp.float32)
    if cuts:
        result = result * block_scale(own_key, shape, cuts, -0.22, 0.18)
    return jnp.clip(with_spikes(result, jax.random.fold_in(own_key, 3), *heavy), -bound, bound).astype(kind)


def setup_inputs(seed: int = 0) -> dict:
    streams_of = jax.random.split(jax.random.key(seed), 8)
    return {
        "hidden_in": heavy_noise(streams_of[0], (TOKENS, MODEL_WIDTH), 1.0, 6.0, ((0, 8),), (0, 1, 8, 2.0)),
        "queries": draw_queries(jax.random.fold_in(streams_of[7], 71), 0),
        "keys": draw_keys(jax.random.fold_in(streams_of[7], 71), 0),
        "value_weight": centred(streams_of[3], (MODEL_WIDTH, KEY_VALUE_HEADS * HEAD_SIZE), MODEL_WIDTH ** -0.5, 0.0625, ((0, 8), (1, 4))),
        "context_grad": centred(streams_of[4], (TOKENS, QUERY_HEADS * HEAD_SIZE), 1.0, 6.0, ((0, 8), (1, 4))),
        "doc_ids": jax.vmap(lambda own: jnp.searchsorted(jnp.cumsum(ragged(own, REPLICA_TOKENS // 16, REPLICA_TOKENS, REPLICA_TOKENS // 2, 2)), jnp.arange(REPLICA_TOKENS), side="right"))(jax.random.split(streams_of[5], N_DP)).reshape((N_DP, REPLICA_TOKENS)).astype(jnp.int32),
        "token_counts": draw_token_counts(jax.random.fold_in(streams_of[7], 71), 0),
    }


def reference(hidden_in, queries, keys, value_weight, context_grad, doc_ids, token_counts):
    query_group = QUERY_HEADS // KEY_VALUE_HEADS
    scale = 1.0 / math.sqrt(HEAD_SIZE)
    counts_f = token_counts.astype(jnp.float32)
    total = jnp.sum(counts_f)
    x_rep = hidden_in.reshape(N_DP, REPLICA_TOKENS, MODEL_WIDTH)
    q_rep = queries.reshape(N_DP, REPLICA_TOKENS, QUERY_HEADS * HEAD_SIZE)
    key_repeated = keys.reshape(N_DP, REPLICA_TOKENS, KEY_VALUE_HEADS * HEAD_SIZE)
    g_rep = context_grad.reshape(N_DP, REPLICA_TOKENS, QUERY_HEADS * HEAD_SIZE)
    position = jnp.arange(REPLICA_TOKENS, dtype=jnp.int32)

    def replica(acc, item):
        x_here, query_local, key_local, g_here, doc_here, count_here = item
        value_states = jnp.dot(x_here, value_weight, preferred_element_type=jnp.float32).astype(jnp.bfloat16)
        query_four_axes = query_local.reshape(REPLICA_TOKENS, KEY_VALUE_HEADS, query_group, HEAD_SIZE).astype(jnp.float32)
        key_three_axes = key_local.reshape(REPLICA_TOKENS, KEY_VALUE_HEADS, HEAD_SIZE).astype(jnp.float32)
        scores = jnp.einsum('ikgd,jkd->kgij', query_four_axes, key_three_axes) * scale
        allowed = (position[None, :] <= position[:, None]) & (doc_here[:, None] == doc_here[None, :])
        scores = jnp.where(allowed, scores, -jnp.inf)
        top = lax.optimization_barrier(jnp.max(scores, axis=-1, keepdims=True))
        expo = jnp.exp(scores - top)
        probs = (expo / lax.optimization_barrier(jnp.sum(expo, axis=-1, keepdims=True))).astype(jnp.bfloat16)
        value_three_axes = value_states.reshape(REPLICA_TOKENS, KEY_VALUE_HEADS, HEAD_SIZE).astype(jnp.float32)
        ctx = jnp.einsum('kgij,jkd->ikgd', probs.astype(jnp.float32), value_three_axes)
        ctx = ctx.astype(jnp.bfloat16).reshape(REPLICA_TOKENS, QUERY_HEADS * HEAD_SIZE)
        valid = position < count_here
        masked_scores = jnp.where(valid[:, None], g_here, jnp.zeros_like(g_here))
        masked_scores = masked_scores.reshape(REPLICA_TOKENS, KEY_VALUE_HEADS, query_group, HEAD_SIZE).astype(jnp.float32)
        value_gradient = jnp.einsum('kgij,ikgd->jkd', probs.astype(jnp.float32), masked_scores)
        value_gradient = value_gradient.astype(jnp.bfloat16).reshape(REPLICA_TOKENS, KEY_VALUE_HEADS * HEAD_SIZE)
        term = jnp.dot(x_here.T, value_gradient, preferred_element_type=jnp.float32)
        return (acc + term * count_here.astype(jnp.float32), ctx)
    start_index = jnp.zeros((MODEL_WIDTH, KEY_VALUE_HEADS * HEAD_SIZE), jnp.float32)
    acc, ctx_all = lax.scan(replica, start_index, (x_rep, q_rep, key_repeated, g_rep, doc_ids, token_counts))
    return (ctx_all.reshape(TOKENS, QUERY_HEADS * HEAD_SIZE), acc / total)
```

```python
import functools
import math

import jax
import jax.numpy as jnp
from jax import lax
from jax.experimental import pallas as pl
from jax.experimental.pallas import tpu as pltpu
from jax.sharding import PartitionSpec as P

QUERY_HEADS = 64
KEY_VALUE_HEADS = 8
HEAD_SIZE = 128
GROUP = QUERY_HEADS // KEY_VALUE_HEADS
MESH = pl.DeviceIdType.MESH
F32 = jnp.float32
BF16 = jnp.bfloat16


def plain(hidden_in, queries, keys, value_weight, context_grad, doc_ids, token_counts):
    tok_rows = hidden_in.shape[0]
    kv_cols = keys.shape[1]
    kv_local = kv_cols // HEAD_SIZE
    scale = 1.0 / math.sqrt(HEAD_SIZE)
    whole = lax.all_gather(value_weight, "dp", axis=0, tiled=True)
    value_states = jnp.dot(hidden_in, whole, preferred_element_type=F32).astype(BF16)
    query_four_axes = queries.reshape(tok_rows, kv_local, GROUP, HEAD_SIZE)
    key_three_axes = keys.reshape(tok_rows, kv_local, HEAD_SIZE)
    scores = (
        jnp.einsum("ikgd,jkd->kgij", query_four_axes, key_three_axes, preferred_element_type=F32)
        * scale
    )
    position = jnp.arange(tok_rows, dtype=jnp.int32)
    doc_here = doc_ids[0]
    allowed = (position[None, :] <= position[:, None]) & (doc_here[:, None] == doc_here[None, :])
    scores = jnp.where(allowed, scores, -jnp.inf)
    top = jnp.max(scores, axis=-1, keepdims=True)
    expo = jnp.exp(scores - top)
    probs = (expo / jnp.sum(expo, axis=-1, keepdims=True)).astype(BF16)
    value_three_axes = value_states.reshape(tok_rows, kv_local, HEAD_SIZE)
    ctx = jnp.einsum("kgij,jkd->ikgd", probs, value_three_axes, preferred_element_type=F32)
    context = ctx.astype(BF16).reshape(tok_rows, kv_local * GROUP * HEAD_SIZE)
    count_here = token_counts[0]
    valid = position < count_here
    masked = jnp.where(valid[:, None], context_grad, jnp.zeros_like(context_grad))
    masked = masked.reshape(tok_rows, kv_local, GROUP, HEAD_SIZE)
    value_gradient = jnp.einsum("kgij,ikgd->jkd", probs, masked, preferred_element_type=F32)
    value_gradient = value_gradient.astype(BF16).reshape(tok_rows, kv_cols)
    count_float = count_here.astype(F32)
    factor = count_float / lax.psum(count_float, "dp")
    full_term = (
        jnp.einsum("tr,tc->rc", hidden_in, value_gradient, preferred_element_type=F32) * factor
    )
    grad = lax.psum_scatter(full_term, "dp", scatter_dimension=0, tiled=True)
    return (context, grad)


def dot_tt(a, b):
    return lax.dot_general(a, b, (((0,), (0,)), ((), ())), preferred_element_type=F32)


def fused_kernel(
    x_hbm, q_hbm, k_hbm, w_hbm, g_hbm, doc_ref, cnt_ref, ctx_hbm, dw_hbm,
    x, xp, q, k, g, wg, pt, bias, dv, dvp, vown, vsend, vrecv, sendbuf, recvbuf, acc, ctx, cnts,
    lsem, xs, xr, ws, wr, cs, cr, ds, dr, vs, vr, ss, sr,
):
    me = lax.axis_index("dp")
    core = lax.rem(me, 2)
    chip = me // 2
    cx = lax.rem(chip, 2)
    cy = chip // 2
    peer = me + 1 - 2 * core
    T, C = k.shape
    R = w_hbm.shape[0]
    kv = C // HEAD_SIZE
    scale = 1.0 / math.sqrt(HEAD_SIZE)

    def chip_at(rel):
        ax = 1 - cx if rel % 2 else cx
        ay = 1 - cy if rel // 2 else cy
        return 2 * ay + ax

    def same(rel):
        return 2 * chip_at(rel) + core

    def cross(rel):
        return 2 * chip_at(rel) + 1 - core

    others = [same(r) for r in (1, 2, 3)] + [cross(r) for r in range(4)]

    lk = pltpu.make_async_copy(k_hbm, k, lsem.at[0])
    lq = pltpu.make_async_copy(q_hbm, q, lsem.at[1])
    lg = pltpu.make_async_copy(g_hbm, g, lsem.at[2])
    lx = pltpu.make_async_copy(x_hbm, x, lsem.at[3])
    lw = pltpu.make_async_copy(w_hbm, wg.at[0], lsem.at[4])
    for c in (lk, lq, lg, lx, lw):
        c.start()

    count = cnt_ref[0].astype(F32)
    cnts[0] = jnp.full(cnts.shape[1:], count, F32)

    bar = pltpu.get_barrier_semaphore()
    for d in others:
        pl.semaphore_signal(bar, inc=1, device_id={"dp": d}, device_id_type=MESH)
    pl.semaphore_wait(bar, len(others))

    def remote(src, dst, s, r, dev):
        c = pltpu.make_async_remote_copy(
            src_ref=src, dst_ref=dst, send_sem=s, recv_sem=r,
            device_id={"dp": dev}, device_id_type=MESH,
        )
        c.start()
        return c

    wcopies = {}
    for rel in (3, 1, 2):
        wcopies[rel] = remote(w_hbm, wg.at[rel], ws.at[rel - 1], wr.at[rel - 1], same(rel))
    ccopies = []
    for i, d in enumerate(others):
        ccopies.append(remote(cnts.at[0], cnts.at[i + 1], cs.at[i], cr.at[i], d))
    xcopies = []
    for rel in range(4):
        cols = pl.ds(pl.multiple_of(cross(rel) * R, R), R)
        xcopies.append(remote(x_hbm.at[:, cols], xp.at[rel], xs.at[rel], xr.at[rel], peer))

    docs = jnp.broadcast_to(doc_ref[...].astype(F32), (T, T))
    jj = lax.broadcasted_iota(jnp.int32, (T, T), 0)
    ii = lax.broadcasted_iota(jnp.int32, (T, T), 1)
    allowed = (jj <= ii) & (docs == docs.T)
    bias[...] = jnp.where(allowed, 0.0, -jnp.inf).astype(F32)
    lk.wait()
    lq.wait()
    lg.wait()
    row = lax.broadcasted_iota(jnp.int32, (T, HEAD_SIZE), 0).astype(F32)

    def group(kh, _):
        kcols = pl.ds(pl.multiple_of(kh * HEAD_SIZE, HEAD_SIZE), HEAD_SIZE)
        keyg = k[:, kcols]
        total = jnp.zeros((T, HEAD_SIZE), F32)
        for h in range(GROUP):
            cols = pl.ds(pl.multiple_of((kh * GROUP + h) * HEAD_SIZE, HEAD_SIZE), HEAD_SIZE)
            st = lax.dot_general(
                keyg, q[:, cols], (((1,), (1,)), ((), ())), preferred_element_type=F32
            )
            st = st * scale + bias[...]
            e = jnp.exp(st - jnp.max(st, axis=0, keepdims=True))
            p = (e * (1.0 / jnp.sum(e, axis=0, keepdims=True))).astype(BF16)
            pt[kh * GROUP + h] = p
            gm = jnp.where(row < count, g[:, cols].astype(F32), 0.0).astype(BF16)
            total = total + jnp.dot(p, gm, preferred_element_type=F32)
        dv[:, kcols] = total.astype(BF16)
        return 0

    lax.fori_loop(0, kv, group, 0)
    dcopy = remote(dv, dvp, ds, dr, peer)
    lx.wait()
    for c in xcopies:
        c.wait_recv()
    ccopies[3].wait_recv()
    dcopy.wait_recv()
    count_p = cnts[4][0:1, 0:1]
    step = min(256, R)

    def partial(rel, store):
        base = same(rel) * R

        def body(t, _):
            off = pl.multiple_of(t * step, step)
            xa = x[:, pl.ds(pl.multiple_of(base + off, step), step)]
            xb = xp[rel, :, pl.ds(off, step)]
            store(off, dot_tt(xa, dv[...]) * count + dot_tt(xb, dvp[...]) * count_p)
            return 0

        lax.fori_loop(0, R // step, body, 0)

    scopies = {}
    for rel in (3, 1, 2):

        def put(off, val, rel=rel):
            sendbuf[rel - 1, pl.ds(off, step), :] = val.astype(BF16)

        partial(rel, put)
        scopies[rel] = remote(
            sendbuf.at[rel - 1], recvbuf.at[rel - 1], ss.at[rel - 1], sr.at[rel - 1], same(rel)
        )

    def keep(off, val):
        acc[pl.ds(off, step), :] = val

    partial(0, keep)

    lw.wait()
    for rel in (0, 1, 2, 3):
        if rel:
            wcopies[rel].wait_recv()
        cols = pl.ds(pl.multiple_of(same(rel) * R, R), R)
        a = jnp.dot(x[:, cols], wg[rel], preferred_element_type=F32)
        b = jnp.dot(xp[rel], wg[rel], preferred_element_type=F32)
        if rel == 0:
            vown[...] = a
            vsend[...] = b
        else:
            vown[...] += a
            vsend[...] += b
    vcopy = remote(vsend, vrecv, vs, vr, peer)
    vcopy.wait_recv()
    vown[...] += vrecv[...]

    def contexts(kh, _):
        kcols = pl.ds(pl.multiple_of(kh * HEAD_SIZE, HEAD_SIZE), HEAD_SIZE)
        val = vown[:, kcols].astype(BF16)
        for h in range(GROUP):
            cols = pl.ds(pl.multiple_of((kh * GROUP + h) * HEAD_SIZE, HEAD_SIZE), HEAD_SIZE)
            ctx[:, cols] = dot_tt(pt[kh * GROUP + h], val).astype(BF16)
        return 0

    lax.fori_loop(0, kv, contexts, 0)
    octx = pltpu.make_async_copy(ctx, ctx_hbm, lsem.at[5])
    octx.start()

    for i, c in enumerate(ccopies):
        if i != 3:
            c.wait_recv()
    whole = cnts[0]
    for i in range(1, len(others) + 1):
        whole = whole + cnts[i]
    inv = 1.0 / whole[0:1, 0:1]
    for rel in (1, 2, 3):
        scopies[rel].wait_recv()
    acc[...] = (
        acc[...] + recvbuf[0].astype(F32) + recvbuf[1].astype(F32) + recvbuf[2].astype(F32)
    ) * inv
    odw = pltpu.make_async_copy(acc, dw_hbm, lsem.at[6])
    odw.start()
    for c in list(wcopies.values()) + ccopies + xcopies + [dcopy, vcopy] + list(scopies.values()):
        c.wait_send()
    octx.wait()
    odw.wait()


def fused(hidden_in, queries, keys, value_weight, context_grad, doc_ids, token_counts):
    T, M = hidden_in.shape
    C = keys.shape[1]
    Q = queries.shape[1]
    R = value_weight.shape[0]
    heads = Q // HEAD_SIZE
    anyspec = pl.BlockSpec(memory_space=pl.ANY)
    hbm = pl.BlockSpec(memory_space=pltpu.HBM)
    dma = pltpu.SemaphoreType.DMA
    return tuple(
        pl.pallas_call(
            fused_kernel,
            out_shape=(
                jax.ShapeDtypeStruct((T, Q), BF16),
                jax.ShapeDtypeStruct((R, C), F32),
            ),
            in_specs=[hbm] * 5
            + [pl.BlockSpec(memory_space=pltpu.VMEM), pl.BlockSpec(memory_space=pltpu.SMEM)],
            out_specs=(anyspec, anyspec),
            scratch_shapes=[
                pltpu.VMEM((T, M), BF16),
                pltpu.VMEM((4, T, R), BF16),
                pltpu.VMEM((T, Q), BF16),
                pltpu.VMEM((T, C), BF16),
                pltpu.VMEM((T, Q), BF16),
                pltpu.VMEM((4, R, C), BF16),
                pltpu.VMEM((heads, T, T), BF16),
                pltpu.VMEM((T, T), F32),
                pltpu.VMEM((T, C), BF16),
                pltpu.VMEM((T, C), BF16),
                pltpu.VMEM((T, C), F32),
                pltpu.VMEM((T, C), F32),
                pltpu.VMEM((T, C), F32),
                pltpu.VMEM((3, R, C), BF16),
                pltpu.VMEM((3, R, C), BF16),
                pltpu.VMEM((R, C), F32),
                pltpu.VMEM((T, Q), BF16),
                pltpu.VMEM((8, 8, 128), F32),
                dma((7,)),
                dma((4,)), dma((4,)),
                dma((3,)), dma((3,)),
                dma((7,)), dma((7,)),
                dma, dma, dma, dma,
                dma((3,)), dma((3,)),
            ],
            compiler_params=pltpu.CompilerParams(
                collective_id=0, has_side_effects=True, vmem_limit_bytes=48 * 1024 * 1024
            ),
        )(hidden_in, queries, keys, value_weight, context_grad, doc_ids, token_counts)
    )


def solution(mesh):
    in_specs = (
        P("dp", None),
        P("dp", "tensor"),
        P("dp", "tensor"),
        P("dp", "tensor"),
        P("dp", "tensor"),
        P("dp", None),
        P("dp"),
    )
    out_specs = (P("dp", "tensor"), P("dp", "tensor"))
    body = fused if mesh.shape["dp"] == 8 else plain
    return jax.shard_map(body, mesh=mesh, in_specs=in_specs, out_specs=out_specs, check_vma=False)
```

```python
import functools
import math

import jax
import jax.numpy as jnp
from jax import lax
from jax.experimental import pallas as pl
from jax.experimental.pallas import tpu as pltpu
from jax.sharding import PartitionSpec as P

QUERY_HEADS = 64
KEY_VALUE_HEADS = 8
HEAD_SIZE = 128
GROUP = QUERY_HEADS // KEY_VALUE_HEADS
MESH = pl.DeviceIdType.MESH
F32 = jnp.float32
BF16 = jnp.bfloat16


def plain(hidden_in, queries, keys, value_weight, context_grad, doc_ids, token_counts):
    tok_rows = hidden_in.shape[0]
    kv_cols = keys.shape[1]
    kv_local = kv_cols // HEAD_SIZE
    scale = 1.0 / math.sqrt(HEAD_SIZE)
    whole = lax.all_gather(value_weight, "dp", axis=0, tiled=True)
    value_states = jnp.dot(hidden_in, whole, preferred_element_type=F32).astype(BF16)
    query_four_axes = queries.reshape(tok_rows, kv_local, GROUP, HEAD_SIZE)
    key_three_axes = keys.reshape(tok_rows, kv_local, HEAD_SIZE)
    scores = (
        jnp.einsum("ikgd,jkd->kgij", query_four_axes, key_three_axes, preferred_element_type=F32)
        * scale
    )
    position = jnp.arange(tok_rows, dtype=jnp.int32)
    doc_here = doc_ids[0]
    allowed = (position[None, :] <= position[:, None]) & (doc_here[:, None] == doc_here[None, :])
    scores = jnp.where(allowed, scores, -jnp.inf)
    top = jnp.max(scores, axis=-1, keepdims=True)
    expo = jnp.exp(scores - top)
    probs = (expo / jnp.sum(expo, axis=-1, keepdims=True)).astype(BF16)
    value_three_axes = value_states.reshape(tok_rows, kv_local, HEAD_SIZE)
    ctx = jnp.einsum("kgij,jkd->ikgd", probs, value_three_axes, preferred_element_type=F32)
    context = ctx.astype(BF16).reshape(tok_rows, kv_local * GROUP * HEAD_SIZE)
    count_here = token_counts[0]
    valid = position < count_here
    masked = jnp.where(valid[:, None], context_grad, jnp.zeros_like(context_grad))
    masked = masked.reshape(tok_rows, kv_local, GROUP, HEAD_SIZE)
    value_gradient = jnp.einsum("kgij,ikgd->jkd", probs, masked, preferred_element_type=F32)
    value_gradient = value_gradient.astype(BF16).reshape(tok_rows, kv_cols)
    count_float = count_here.astype(F32)
    factor = count_float / lax.psum(count_float, "dp")
    full_term = (
        jnp.einsum("tr,tc->rc", hidden_in, value_gradient, preferred_element_type=F32) * factor
    )
    grad = lax.psum_scatter(full_term, "dp", scatter_dimension=0, tiled=True)
    return (context, grad)


def dot_tt(a, b):
    return lax.dot_general(a, b, (((0,), (0,)), ((), ())), preferred_element_type=F32)


def fused_kernel(
    x_hbm, q_hbm, k_hbm, w_hbm, g_hbm, doc_ref, cnt_ref, ctx, dw_ref,
    x, xp, q, k, g, wg, pt, bias, dv, dvp, vown, vsend, vrecv, sendbuf, recvbuf, acc, cnts,
    lsem, xs, xr, ws, wr, cs, cr, ds, dr, vs, vr, ss, sr,
):
    me = lax.axis_index("dp")
    core = lax.rem(me, 2)
    chip = me // 2
    cx = lax.rem(chip, 2)
    cy = chip // 2
    peer = me + 1 - 2 * core
    T, C = k.shape
    R = w_hbm.shape[0]
    kv = C // HEAD_SIZE
    scale = 1.0 / math.sqrt(HEAD_SIZE)

    def chip_at(rel):
        ax = 1 - cx if rel % 2 else cx
        ay = 1 - cy if rel // 2 else cy
        return 2 * ay + ax

    def same(rel):
        return 2 * chip_at(rel) + core

    def cross(rel):
        return 2 * chip_at(rel) + 1 - core

    others = [same(r) for r in (1, 2, 3)] + [cross(r) for r in range(4)]

    lk = pltpu.make_async_copy(k_hbm, k, lsem.at[0])
    lq = pltpu.make_async_copy(q_hbm, q, lsem.at[1])
    lg = pltpu.make_async_copy(g_hbm, g, lsem.at[2])
    lx = pltpu.make_async_copy(x_hbm, x, lsem.at[3])
    lw = pltpu.make_async_copy(w_hbm, wg.at[0], lsem.at[4])
    for c in (lk, lq, lg, lx, lw):
        c.start()

    count = cnt_ref[0].astype(F32)
    cnts[0] = jnp.full(cnts.shape[1:], count, F32)

    bar = pltpu.get_barrier_semaphore()
    for d in others:
        pl.semaphore_signal(bar, inc=1, device_id={"dp": d}, device_id_type=MESH)
    pl.semaphore_wait(bar, len(others))

    def remote(src, dst, s, r, dev):
        c = pltpu.make_async_remote_copy(
            src_ref=src, dst_ref=dst, send_sem=s, recv_sem=r,
            device_id={"dp": dev}, device_id_type=MESH,
        )
        c.start()
        return c

    H = R // 2
    half = (pl.ds(0, H), pl.ds(H, H))

    def own_half(rel, part):
        i = 2 * (rel - 1) + part
        return remote(
            w_hbm.at[half[part]], wg.at[rel, half[part]], ws.at[i], wr.at[i], same(rel)
        )

    def onward(src, part):
        i = 4 + part
        return remote(
            wg.at[src, half[part]], wg.at[3, half[part]], ws.at[i], wr.at[i], same(3 - src)
        )

    wx0, wy1 = own_half(1, 0), own_half(2, 1)
    wx1, wy0 = own_half(1, 1), own_half(2, 0)
    ccopies = []
    for i, d in enumerate(others):
        ccopies.append(remote(cnts.at[0], cnts.at[i + 1], cs.at[i], cr.at[i], d))
    xcopies = []
    for rel in range(4):
        cols = pl.ds(pl.multiple_of(cross(rel) * R, R), R)
        xcopies.append(remote(x_hbm.at[:, cols], xp.at[rel], xs.at[rel], xr.at[rel], peer))

    docs = jnp.broadcast_to(doc_ref[...].astype(F32), (T, T))
    jj = lax.broadcasted_iota(jnp.int32, (T, T), 0)
    ii = lax.broadcasted_iota(jnp.int32, (T, T), 1)
    allowed = (jj <= ii) & (docs == docs.T)
    bias[...] = jnp.where(allowed, 0.0, -jnp.inf).astype(F32)
    lk.wait()
    lq.wait()
    lg.wait()
    row = lax.broadcasted_iota(jnp.int32, (T, HEAD_SIZE), 0).astype(F32)

    def group(kh, _):
        kcols = pl.ds(pl.multiple_of(kh * HEAD_SIZE, HEAD_SIZE), HEAD_SIZE)
        keyg = k[:, kcols]
        total = jnp.zeros((T, HEAD_SIZE), F32)
        for h in range(GROUP):
            cols = pl.ds(pl.multiple_of((kh * GROUP + h) * HEAD_SIZE, HEAD_SIZE), HEAD_SIZE)
            st = lax.dot_general(
                keyg, q[:, cols], (((1,), (1,)), ((), ())), preferred_element_type=F32
            )
            st = st * scale + bias[...]
            e = jnp.exp(st - jnp.max(st, axis=0, keepdims=True))
            p = (e * (1.0 / jnp.sum(e, axis=0, keepdims=True))).astype(BF16)
            pt[kh * GROUP + h] = p
            gm = jnp.where(row < count, g[:, cols].astype(F32), 0.0).astype(BF16)
            total = total + jnp.dot(p, gm, preferred_element_type=F32)
        dv[:, kcols] = total.astype(BF16)
        return 0

    split = kv // 2
    lax.fori_loop(0, split, group, 0)
    wx0.wait_recv()
    fy0 = onward(1, 0)
    wy1.wait_recv()
    fx1 = onward(2, 1)
    lax.fori_loop(split, kv, group, 0)
    dcopy = remote(dv, dvp, ds, dr, peer)
    lx.wait()
    for c in xcopies:
        c.wait_recv()
    ccopies[3].wait_recv()
    dcopy.wait_recv()
    count_p = cnts[4][0:1, 0:1]
    step = min(256, H)

    def partial(rel, part, store):
        base = same(rel) * R
        first = part * H

        def body(t, _):
            off = pl.multiple_of(first + t * step, step)
            xa = x[:, pl.ds(pl.multiple_of(base + off, step), step)]
            xb = xp[rel, :, pl.ds(off, step)]
            store(off, dot_tt(xa, dv[...]) * count + dot_tt(xb, dvp[...]) * count_p)
            return 0

        lax.fori_loop(0, H // step, body, 0)

    def ship(slot, rel, part, to, add=None):
        def put(off, val):
            here = pl.ds(off - part * H, step)
            if add is not None:
                val = val + recvbuf[add, here, :].astype(F32)
            sendbuf[slot, here, :] = val.astype(BF16)

        partial(rel, part, put)
        return remote(sendbuf.at[slot], recvbuf.at[slot], ss.at[slot], sr.at[slot], same(to))

    def keep(off, val):
        acc[pl.ds(off, step), :] = val

    scopies = [ship(0, 3, 0, 1), ship(1, 3, 1, 2), ship(2, 1, 0, 1), ship(3, 2, 1, 2)]
    partial(0, 0, keep)
    scopies[1].wait_recv()
    scopies.append(ship(4, 1, 1, 1, add=1))
    scopies[0].wait_recv()
    scopies.append(ship(5, 2, 0, 2, add=0))
    partial(0, 1, keep)

    lw.wait()
    for rel in (0, 1, 2, 3):
        for c in ((), (wx1,), (wy0,), (fy0, fx1))[rel]:
            c.wait_recv()
        cols = pl.ds(pl.multiple_of(same(rel) * R, R), R)
        a = jnp.dot(x[:, cols], wg[rel], preferred_element_type=F32)
        b = jnp.dot(xp[rel], wg[rel], preferred_element_type=F32)
        if rel == 0:
            vown[...] = a
            vsend[...] = b
        else:
            vown[...] += a
            vsend[...] += b
    vcopy = remote(vsend, vrecv, vs, vr, peer)
    vcopy.wait_recv()
    vown[...] += vrecv[...]

    def contexts(kh, _):
        kcols = pl.ds(pl.multiple_of(kh * HEAD_SIZE, HEAD_SIZE), HEAD_SIZE)
        val = vown[:, kcols].astype(BF16)
        for h in range(GROUP):
            cols = pl.ds(pl.multiple_of((kh * GROUP + h) * HEAD_SIZE, HEAD_SIZE), HEAD_SIZE)
            ctx[:, cols] = dot_tt(pt[kh * GROUP + h], val).astype(BF16)
        return 0

    lax.fori_loop(0, kv, contexts, 0)

    for i, c in enumerate(ccopies):
        if i != 3:
            c.wait_recv()
    whole = cnts[0]
    for i in range(1, len(others) + 1):
        whole = whole + cnts[i]
    inv = 1.0 / whole[0:1, 0:1]
    for i in (2, 3, 4, 5):
        scopies[i].wait_recv()
    for part, (one, two) in ((0, (2, 5)), (1, (3, 4))):
        dw_ref[half[part], :] = (
            acc[half[part], :] + recvbuf[one].astype(F32) + recvbuf[two].astype(F32)
        ) * inv
    for c in [wx0, wx1, wy0, wy1, fx1, fy0, dcopy, vcopy] + ccopies + xcopies + scopies:
        c.wait_send()


def fused(hidden_in, queries, keys, value_weight, context_grad, doc_ids, token_counts):
    T, M = hidden_in.shape
    C = keys.shape[1]
    Q = queries.shape[1]
    R = value_weight.shape[0]
    heads = Q // HEAD_SIZE
    hbm = pl.BlockSpec(memory_space=pltpu.HBM)
    dma = pltpu.SemaphoreType.DMA
    pinned = [
        pltpu.with_memory_space_constraint(a, pltpu.HBM)
        for a in (hidden_in, queries, keys, value_weight, context_grad)
    ]
    return tuple(
        pl.pallas_call(
            fused_kernel,
            out_shape=(
                jax.ShapeDtypeStruct((T, Q), BF16),
                jax.ShapeDtypeStruct((R, C), F32),
            ),
            in_specs=[hbm] * 5
            + [pl.BlockSpec(memory_space=pltpu.VMEM), pl.BlockSpec(memory_space=pltpu.SMEM)],
            out_specs=(pl.BlockSpec(memory_space=pltpu.VMEM),) * 2,
            scratch_shapes=[
                pltpu.VMEM((T, M), BF16),
                pltpu.VMEM((4, T, R), BF16),
                pltpu.VMEM((T, Q), BF16),
                pltpu.VMEM((T, C), BF16),
                pltpu.VMEM((T, Q), BF16),
                pltpu.VMEM((4, R, C), BF16),
                pltpu.VMEM((heads, T, T), BF16),
                pltpu.VMEM((T, T), F32),
                pltpu.VMEM((T, C), BF16),
                pltpu.VMEM((T, C), BF16),
                pltpu.VMEM((T, C), F32),
                pltpu.VMEM((T, C), F32),
                pltpu.VMEM((T, C), F32),
                pltpu.VMEM((6, R // 2, C), BF16),
                pltpu.VMEM((6, R // 2, C), BF16),
                pltpu.VMEM((R, C), F32),
                pltpu.VMEM((8, 8, 128), F32),
                dma((5,)),
                dma((4,)), dma((4,)),
                dma((6,)), dma((6,)),
                dma((7,)), dma((7,)),
                dma, dma, dma, dma,
                dma((6,)), dma((6,)),
            ],
            compiler_params=pltpu.CompilerParams(
                collective_id=0, has_side_effects=True, vmem_limit_bytes=48 * 1024 * 1024
            ),
        )(*pinned, doc_ids, token_counts)
    )


def solution(mesh):
    in_specs = (
        P("dp", None),
        P("dp", "tensor"),
        P("dp", "tensor"),
        P("dp", "tensor"),
        P("dp", "tensor"),
        P("dp", None),
        P("dp"),
    )
    out_specs = (P("dp", "tensor"), P("dp", "tensor"))
    body = fused if mesh.shape["dp"] == 8 else plain
    return jax.shard_map(body, mesh=mesh, in_specs=in_specs, out_specs=out_specs, check_vma=False)
```

```python
import functools
import math

import jax
import jax.numpy as jnp
from jax import lax
from jax.experimental import pallas as pl
from jax.experimental.pallas import tpu as pltpu
from jax.sharding import PartitionSpec as P

QUERY_HEADS = 64
KEY_VALUE_HEADS = 8
HEAD_SIZE = 128
GROUP = QUERY_HEADS // KEY_VALUE_HEADS
MESH = pl.DeviceIdType.MESH
F32 = jnp.float32
BF16 = jnp.bfloat16


def plain(hidden_in, queries, keys, value_weight, context_grad, doc_ids, token_counts):
    tok_rows = hidden_in.shape[0]
    kv_cols = keys.shape[1]
    kv_local = kv_cols // HEAD_SIZE
    scale = 1.0 / math.sqrt(HEAD_SIZE)
    whole = lax.all_gather(value_weight, "dp", axis=0, tiled=True)
    value_states = jnp.dot(hidden_in, whole, preferred_element_type=F32).astype(BF16)
    query_four_axes = queries.reshape(tok_rows, kv_local, GROUP, HEAD_SIZE)
    key_three_axes = keys.reshape(tok_rows, kv_local, HEAD_SIZE)
    scores = (
        jnp.einsum("ikgd,jkd->kgij", query_four_axes, key_three_axes, preferred_element_type=F32)
        * scale
    )
    position = jnp.arange(tok_rows, dtype=jnp.int32)
    doc_here = doc_ids[0]
    allowed = (position[None, :] <= position[:, None]) & (doc_here[:, None] == doc_here[None, :])
    scores = jnp.where(allowed, scores, -jnp.inf)
    top = jnp.max(scores, axis=-1, keepdims=True)
    expo = jnp.exp(scores - top)
    probs = (expo / jnp.sum(expo, axis=-1, keepdims=True)).astype(BF16)
    value_three_axes = value_states.reshape(tok_rows, kv_local, HEAD_SIZE)
    ctx = jnp.einsum("kgij,jkd->ikgd", probs, value_three_axes, preferred_element_type=F32)
    context = ctx.astype(BF16).reshape(tok_rows, kv_local * GROUP * HEAD_SIZE)
    count_here = token_counts[0]
    valid = position < count_here
    masked = jnp.where(valid[:, None], context_grad, jnp.zeros_like(context_grad))
    masked = masked.reshape(tok_rows, kv_local, GROUP, HEAD_SIZE)
    value_gradient = jnp.einsum("kgij,ikgd->jkd", probs, masked, preferred_element_type=F32)
    value_gradient = value_gradient.astype(BF16).reshape(tok_rows, kv_cols)
    count_float = count_here.astype(F32)
    factor = count_float / lax.psum(count_float, "dp")
    full_term = (
        jnp.einsum("tr,tc->rc", hidden_in, value_gradient, preferred_element_type=F32) * factor
    )
    grad = lax.psum_scatter(full_term, "dp", scatter_dimension=0, tiled=True)
    return (context, grad)


def dot_tt(a, b):
    return lax.dot_general(a, b, (((0,), (0,)), ((), ())), preferred_element_type=F32)


def fused_kernel(
    x_hbm, q_hbm, k_hbm, w_hbm, g_hbm, doc_hbm, cnt_ref, ctx, dw_ref,
    x, xp, q, k, g, wg, pt, bias, dv, dvp, vown, vsend, vrecv, sendbuf, recvbuf, acc, cnts, doc_ref,
    lsem, xs, xr, ws, wr, cs, cr, ds, dr, vs, vr, ss, sr,
):
    me = lax.axis_index("dp")
    core = lax.rem(me, 2)
    chip = me // 2
    cx = lax.rem(chip, 2)
    cy = chip // 2
    peer = me + 1 - 2 * core
    T, C = k.shape
    R = w_hbm.shape[0]
    kv = C // HEAD_SIZE
    scale = 1.0 / math.sqrt(HEAD_SIZE)

    def chip_at(rel):
        ax = 1 - cx if rel % 2 else cx
        ay = 1 - cy if rel // 2 else cy
        return 2 * ay + ax

    def same(rel):
        return 2 * chip_at(rel) + core

    def cross(rel):
        return 2 * chip_at(rel) + 1 - core

    others = (peer, same(1), same(2))

    lk = pltpu.make_async_copy(k_hbm, k, lsem.at[0])
    lq = pltpu.make_async_copy(q_hbm, q, lsem.at[1])
    lg = pltpu.make_async_copy(g_hbm, g, lsem.at[2])
    lx = pltpu.make_async_copy(x_hbm, x, lsem.at[3])
    lw = pltpu.make_async_copy(w_hbm, wg.at[0], lsem.at[4])
    ld = pltpu.make_async_copy(doc_hbm, doc_ref, lsem.at[5])
    for c in (ld, lk, lq, lg, lx, lw):
        c.start()

    bar = pltpu.get_barrier_semaphore()
    for d in others:
        pl.semaphore_signal(bar, inc=1, device_id={"dp": d}, device_id_type=MESH)
    pl.semaphore_wait(bar, len(others))

    def remote(src, dst, s, r, dev):
        c = pltpu.make_async_remote_copy(
            src_ref=src, dst_ref=dst, send_sem=s, recv_sem=r,
            device_id={"dp": dev}, device_id_type=MESH,
        )
        c.start()
        return c

    H = R // 2
    half = (pl.ds(0, H), pl.ds(H, H))

    def own_half(rel, part):
        i = 2 * (rel - 1) + part
        return remote(
            w_hbm.at[half[part]], wg.at[rel, half[part]], ws.at[i], wr.at[i], same(rel)
        )

    def onward(src, part):
        i = 4 + part
        return remote(
            wg.at[src, half[part]], wg.at[3, half[part]], ws.at[i], wr.at[i], same(3 - src)
        )

    wx0, wy1 = own_half(1, 0), own_half(2, 1)
    wx1, wy0 = own_half(1, 1), own_half(2, 0)
    count = cnt_ref[0].astype(F32)
    cnts[0] = jnp.full(cnts.shape[1:], count, F32)
    c0 = remote(cnts.at[0], cnts.at[1], cs.at[0], cr.at[0], peer)
    xcopies = []
    for rel in range(4):
        cols = pl.ds(pl.multiple_of(cross(rel) * R, R), R)
        xcopies.append(remote(x_hbm.at[:, cols], xp.at[rel], xs.at[rel], xr.at[rel], peer))

    ld.wait()
    docs = jnp.broadcast_to(doc_ref[...].astype(F32), (T, T))
    jj = lax.broadcasted_iota(jnp.int32, (T, T), 0)
    ii = lax.broadcasted_iota(jnp.int32, (T, T), 1)
    allowed = (jj <= ii) & (docs == docs.T)
    bias[...] = jnp.where(allowed, 0.0, -jnp.inf).astype(F32)
    lk.wait()
    lq.wait()
    lg.wait()
    row = lax.broadcasted_iota(jnp.int32, (T, HEAD_SIZE), 0).astype(F32)

    def group(kh, _):
        kcols = pl.ds(pl.multiple_of(kh * HEAD_SIZE, HEAD_SIZE), HEAD_SIZE)
        keyg = k[:, kcols]
        total = jnp.zeros((T, HEAD_SIZE), F32)
        for h in range(GROUP):
            cols = pl.ds(pl.multiple_of((kh * GROUP + h) * HEAD_SIZE, HEAD_SIZE), HEAD_SIZE)
            st = lax.dot_general(
                keyg, q[:, cols], (((1,), (1,)), ((), ())), preferred_element_type=F32
            )
            st = st * scale + bias[...]
            e = jnp.exp(st - jnp.max(st, axis=0, keepdims=True))
            p = (e * (1.0 / jnp.sum(e, axis=0, keepdims=True))).astype(BF16)
            pt[kh * GROUP + h] = p
            gm = jnp.where(row < count, g[:, cols].astype(F32), 0.0).astype(BF16)
            total = total + jnp.dot(p, gm, preferred_element_type=F32)
        dv[:, kcols] = total.astype(BF16)
        return 0

    split = kv // 2
    lax.fori_loop(0, split, group, 0)
    wx0.wait_recv()
    fy0 = onward(1, 0)
    wy1.wait_recv()
    fx1 = onward(2, 1)
    lax.fori_loop(split, kv, group, 0)
    dcopy = remote(dv, dvp, ds, dr, peer)
    lx.wait()
    for c in xcopies:
        c.wait_recv()
    c0.wait_recv()
    dcopy.wait_recv()
    count_p = cnts[1][0:1, 0:1]
    cnts[2] = cnts[0] + cnts[1]
    c1 = remote(cnts.at[2], cnts.at[3], cs.at[1], cr.at[1], same(1))
    step = min(256, H)

    def partial(rel, part, store):
        base = same(rel) * R
        first = part * H

        def body(t, _):
            off = pl.multiple_of(first + t * step, step)
            xa = x[:, pl.ds(pl.multiple_of(base + off, step), step)]
            xb = xp[rel, :, pl.ds(off, step)]
            store(off, dot_tt(xa, dv[...]) * count + dot_tt(xb, dvp[...]) * count_p)
            return 0

        lax.fori_loop(0, H // step, body, 0)

    def ship(slot, rel, part, to, add=None):
        def put(off, val):
            here = pl.ds(off - part * H, step)
            if add is not None:
                val = val + recvbuf[add, here, :].astype(F32)
            sendbuf[slot, here, :] = val.astype(BF16)

        partial(rel, part, put)
        return remote(sendbuf.at[slot], recvbuf.at[slot], ss.at[slot], sr.at[slot], same(to))

    def keep(off, val):
        acc[pl.ds(off, step), :] = val

    scopies = [ship(0, 3, 0, 1), ship(1, 3, 1, 2), ship(2, 1, 0, 1), ship(3, 2, 1, 2)]
    partial(0, 0, keep)
    c1.wait_recv()
    cnts[4] = cnts[2] + cnts[3]
    c2 = remote(cnts.at[4], cnts.at[5], cs.at[2], cr.at[2], same(2))
    scopies[1].wait_recv()
    scopies.append(ship(4, 1, 1, 1, add=1))
    scopies[0].wait_recv()
    scopies.append(ship(5, 2, 0, 2, add=0))
    partial(0, 1, keep)

    lw.wait()
    for rel in (0, 1, 2, 3):
        for c in ((), (wx1,), (wy0,), (fy0, fx1))[rel]:
            c.wait_recv()
        cols = pl.ds(pl.multiple_of(same(rel) * R, R), R)
        a = jnp.dot(x[:, cols], wg[rel], preferred_element_type=F32)
        b = jnp.dot(xp[rel], wg[rel], preferred_element_type=F32)
        if rel == 0:
            vown[...] = a
            vsend[...] = b
        else:
            vown[...] += a
            vsend[...] += b
    vcopy = remote(vsend, vrecv, vs, vr, peer)
    vcopy.wait_recv()
    vown[...] += vrecv[...]

    def contexts(kh, _):
        kcols = pl.ds(pl.multiple_of(kh * HEAD_SIZE, HEAD_SIZE), HEAD_SIZE)
        val = vown[:, kcols].astype(BF16)
        for h in range(GROUP):
            cols = pl.ds(pl.multiple_of((kh * GROUP + h) * HEAD_SIZE, HEAD_SIZE), HEAD_SIZE)
            ctx[:, cols] = dot_tt(pt[kh * GROUP + h], val).astype(BF16)
        return 0

    lax.fori_loop(0, kv, contexts, 0)

    c2.wait_recv()
    inv = 1.0 / (cnts[4] + cnts[5])[0:1, 0:1]
    for part in (0, 1):
        scopies[2 + part].wait_recv()
        acc[half[part], :] += recvbuf[2 + part].astype(F32)
    for part in (1, 0):
        scopies[5 - part].wait_recv()
        dw_ref[half[part], :] = (acc[half[part], :] + recvbuf[5 - part].astype(F32)) * inv
    for c in [wx0, wx1, wy0, wy1, fx1, fy0, dcopy, vcopy, c0, c1, c2] + xcopies + scopies:
        c.wait_send()


def fused(hidden_in, queries, keys, value_weight, context_grad, doc_ids, token_counts):
    T, M = hidden_in.shape
    C = keys.shape[1]
    Q = queries.shape[1]
    R = value_weight.shape[0]
    heads = Q // HEAD_SIZE
    hbm = pl.BlockSpec(memory_space=pltpu.HBM)
    dma = pltpu.SemaphoreType.DMA
    pinned = [
        pltpu.with_memory_space_constraint(a, pltpu.HBM)
        for a in (hidden_in, queries, keys, value_weight, context_grad, doc_ids)
    ]
    return tuple(
        pl.pallas_call(
            fused_kernel,
            out_shape=(
                jax.ShapeDtypeStruct((T, Q), BF16),
                jax.ShapeDtypeStruct((R, C), F32),
            ),
            in_specs=[hbm] * 6 + [pl.BlockSpec(memory_space=pltpu.SMEM)],
            out_specs=(pl.BlockSpec(memory_space=pltpu.VMEM),) * 2,
            scratch_shapes=[
                pltpu.VMEM((T, M), BF16),
                pltpu.VMEM((4, T, R), BF16),
                pltpu.VMEM((T, Q), BF16),
                pltpu.VMEM((T, C), BF16),
                pltpu.VMEM((T, Q), BF16),
                pltpu.VMEM((4, R, C), BF16),
                pltpu.VMEM((heads, T, T), BF16),
                pltpu.VMEM((T, T), F32),
                pltpu.VMEM((T, C), BF16),
                pltpu.VMEM((T, C), BF16),
                pltpu.VMEM((T, C), F32),
                pltpu.VMEM((T, C), F32),
                pltpu.VMEM((T, C), F32),
                pltpu.VMEM((6, R // 2, C), BF16),
                pltpu.VMEM((6, R // 2, C), BF16),
                pltpu.VMEM((R, C), F32),
                pltpu.VMEM((6, 8, 128), F32),
                pltpu.VMEM(doc_ids.shape, jnp.int32),
                dma((6,)),
                dma((4,)), dma((4,)),
                dma((6,)), dma((6,)),
                dma((3,)), dma((3,)),
                dma, dma, dma, dma,
                dma((6,)), dma((6,)),
            ],
            compiler_params=pltpu.CompilerParams(
                collective_id=0, has_side_effects=True, vmem_limit_bytes=48 * 1024 * 1024
            ),
        )(*pinned, token_counts)
    )


def solution(mesh):
    in_specs = (
        P("dp", None),
        P("dp", "tensor"),
        P("dp", "tensor"),
        P("dp", "tensor"),
        P("dp", "tensor"),
        P("dp", None),
        P("dp"),
    )
    out_specs = (P("dp", "tensor"), P("dp", "tensor"))
    body = fused if mesh.shape["dp"] == 8 else plain
    return jax.shard_map(body, mesh=mesh, in_specs=in_specs, out_specs=out_specs, check_vma=False)
```

```python
import functools
import math

import jax
import jax.numpy as jnp
from jax import lax
from jax.experimental import pallas as pl
from jax.experimental.pallas import tpu as pltpu
from jax.sharding import PartitionSpec as P

QUERY_HEADS = 64
KEY_VALUE_HEADS = 8
HEAD_SIZE = 128
GROUP = QUERY_HEADS // KEY_VALUE_HEADS
MESH = pl.DeviceIdType.MESH
F32 = jnp.float32
BF16 = jnp.bfloat16


def plain(hidden_in, queries, keys, value_weight, context_grad, doc_ids, token_counts):
    tok_rows = hidden_in.shape[0]
    kv_cols = keys.shape[1]
    kv_local = kv_cols // HEAD_SIZE
    scale = 1.0 / math.sqrt(HEAD_SIZE)
    whole = lax.all_gather(value_weight, "dp", axis=0, tiled=True)
    value_states = jnp.dot(hidden_in, whole, preferred_element_type=F32).astype(BF16)
    query_four_axes = queries.reshape(tok_rows, kv_local, GROUP, HEAD_SIZE)
    key_three_axes = keys.reshape(tok_rows, kv_local, HEAD_SIZE)
    scores = (
        jnp.einsum("ikgd,jkd->kgij", query_four_axes, key_three_axes, preferred_element_type=F32)
        * scale
    )
    position = jnp.arange(tok_rows, dtype=jnp.int32)
    doc_here = doc_ids[0]
    allowed = (position[None, :] <= position[:, None]) & (doc_here[:, None] == doc_here[None, :])
    scores = jnp.where(allowed, scores, -jnp.inf)
    top = jnp.max(scores, axis=-1, keepdims=True)
    expo = jnp.exp(scores - top)
    probs = (expo / jnp.sum(expo, axis=-1, keepdims=True)).astype(BF16)
    value_three_axes = value_states.reshape(tok_rows, kv_local, HEAD_SIZE)
    ctx = jnp.einsum("kgij,jkd->ikgd", probs, value_three_axes, preferred_element_type=F32)
    context = ctx.astype(BF16).reshape(tok_rows, kv_local * GROUP * HEAD_SIZE)
    count_here = token_counts[0]
    valid = position < count_here
    masked = jnp.where(valid[:, None], context_grad, jnp.zeros_like(context_grad))
    masked = masked.reshape(tok_rows, kv_local, GROUP, HEAD_SIZE)
    value_gradient = jnp.einsum("kgij,ikgd->jkd", probs, masked, preferred_element_type=F32)
    value_gradient = value_gradient.astype(BF16).reshape(tok_rows, kv_cols)
    count_float = count_here.astype(F32)
    factor = count_float / lax.psum(count_float, "dp")
    full_term = (
        jnp.einsum("tr,tc->rc", hidden_in, value_gradient, preferred_element_type=F32) * factor
    )
    grad = lax.psum_scatter(full_term, "dp", scatter_dimension=0, tiled=True)
    return (context, grad)


def dot_tt(a, b):
    return lax.dot_general(a, b, (((0,), (0,)), ((), ())), preferred_element_type=F32)


def fused_kernel(
    x_hbm, q_hbm, k_hbm, w_hbm, g_hbm, doc_hbm, cnt_ref, ctx, dw_ref,
    x, xp, q, k, g, wg, pt, bias, dv, dvp, vown, vsend, vrecv, sendbuf, recvbuf, acc, cnts, doc_ref,
    lsem, xs, xr, ws, wr, cs, cr, ds, dr, vs, vr, ss, sr,
):
    me = lax.axis_index("dp")
    core = lax.rem(me, 2)
    chip = me // 2
    cx = lax.rem(chip, 2)
    cy = chip // 2
    peer = me + 1 - 2 * core
    T, C = k.shape
    R = w_hbm.shape[0]
    kv = C // HEAD_SIZE
    scale = 1.0 / math.sqrt(HEAD_SIZE)

    def chip_at(rel):
        ax = 1 - cx if rel % 2 else cx
        ay = 1 - cy if rel // 2 else cy
        return 2 * ay + ax

    def same(rel):
        return 2 * chip_at(rel) + core

    def cross(rel):
        return 2 * chip_at(rel) + 1 - core

    others = (peer, same(1), same(2))

    lk = pltpu.make_async_copy(k_hbm, k, lsem.at[0])
    lq = pltpu.make_async_copy(q_hbm, q, lsem.at[1])
    lg = pltpu.make_async_copy(g_hbm, g, lsem.at[2])
    lx = pltpu.make_async_copy(x_hbm, x, lsem.at[3])
    lw = pltpu.make_async_copy(w_hbm, wg.at[0], lsem.at[4])
    ld = pltpu.make_async_copy(doc_hbm, doc_ref, lsem.at[5])
    for c in (ld, lk, lq, lg, lx, lw):
        c.start()

    bar = pltpu.get_barrier_semaphore()
    for d in others:
        pl.semaphore_signal(bar, inc=1, device_id={"dp": d}, device_id_type=MESH)
    pl.semaphore_wait(bar, len(others))

    def remote(src, dst, s, r, dev):
        c = pltpu.make_async_remote_copy(
            src_ref=src, dst_ref=dst, send_sem=s, recv_sem=r,
            device_id={"dp": dev}, device_id_type=MESH,
        )
        c.start()
        return c

    H = R // 2
    half = (pl.ds(0, H), pl.ds(H, H))

    def own_half(rel, part):
        i = 2 * (rel - 1) + part
        return remote(
            w_hbm.at[half[part]], wg.at[rel, half[part]], ws.at[i], wr.at[i], same(rel)
        )

    def onward(src, part):
        i = 4 + part
        return remote(
            wg.at[src, half[part]], wg.at[3, half[part]], ws.at[i], wr.at[i], same(3 - src)
        )

    wx0, wy1 = own_half(1, 0), own_half(2, 1)
    wx1, wy0 = own_half(1, 1), own_half(2, 0)
    count = cnt_ref[0].astype(F32)
    cnts[0] = jnp.full(cnts.shape[1:], count, F32)
    c0 = remote(cnts.at[0], cnts.at[1], cs.at[0], cr.at[0], peer)
    xcopies = []
    for rel in range(4):
        cols = pl.ds(pl.multiple_of(cross(rel) * R, R), R)
        xcopies.append(remote(x_hbm.at[:, cols], xp.at[rel], xs.at[rel], xr.at[rel], peer))

    ld.wait()
    docs = jnp.broadcast_to(doc_ref[...].astype(F32), (T, T))
    jj = lax.broadcasted_iota(jnp.int32, (T, T), 0)
    ii = lax.broadcasted_iota(jnp.int32, (T, T), 1)
    allowed = (jj <= ii) & (docs == docs.T)
    bias[...] = jnp.where(allowed, 0.0, -jnp.inf).astype(F32)
    lk.wait()
    lq.wait()
    lg.wait()
    row = lax.broadcasted_iota(jnp.int32, (T, HEAD_SIZE), 0).astype(F32)

    def group(kh, _):
        kcols = pl.ds(pl.multiple_of(kh * HEAD_SIZE, HEAD_SIZE), HEAD_SIZE)
        keyg = k[:, kcols]
        total = jnp.zeros((T, HEAD_SIZE), F32)
        for h in range(GROUP):
            cols = pl.ds(pl.multiple_of((kh * GROUP + h) * HEAD_SIZE, HEAD_SIZE), HEAD_SIZE)
            st = lax.dot_general(
                keyg, q[:, cols], (((1,), (1,)), ((), ())), preferred_element_type=F32
            )
            st = st * scale + bias[...]
            e = jnp.exp(st - jnp.max(st, axis=0, keepdims=True))
            p = (e * (1.0 / jnp.sum(e, axis=0, keepdims=True))).astype(BF16)
            pt[kh * GROUP + h] = p
            gm = jnp.where(row < count, g[:, cols].astype(F32), 0.0).astype(BF16)
            total = total + jnp.dot(p, gm, preferred_element_type=F32)
        dv[:, kcols] = total.astype(BF16)
        return 0

    split = kv // 2
    lax.fori_loop(0, split, group, 0)
    wx0.wait_recv()
    fy0 = onward(1, 0)
    wy1.wait_recv()
    fx1 = onward(2, 1)
    lax.fori_loop(split, kv, group, 0)
    dcopy = remote(dv, dvp, ds, dr, peer)
    lx.wait()
    for c in xcopies:
        c.wait_recv()
    c0.wait_recv()
    dcopy.wait_recv()
    count_p = cnts[1][0:1, 0:1]
    cnts[2] = cnts[0] + cnts[1]
    c1 = remote(cnts.at[2], cnts.at[3], cs.at[1], cr.at[1], same(1))
    step = min(256, H)

    def partial(rel, part, store):
        base = same(rel) * R
        first = part * H

        def body(t, _):
            off = pl.multiple_of(first + t * step, step)
            xa = x[:, pl.ds(pl.multiple_of(base + off, step), step)]
            xb = xp[rel, :, pl.ds(off, step)]
            store(off, dot_tt(xa, dv[...]) * count + dot_tt(xb, dvp[...]) * count_p)
            return 0

        lax.fori_loop(0, H // step, body, 0)

    def ship(slot, rel, part, to, add=None):
        def put(off, val):
            here = pl.ds(off - part * H, step)
            if add is not None:
                val = val + recvbuf[add, here, :].astype(F32)
            sendbuf[slot, here, :] = val.astype(BF16)

        partial(rel, part, put)
        return remote(sendbuf.at[slot], recvbuf.at[slot], ss.at[slot], sr.at[slot], same(to))

    def keep(off, val):
        acc[pl.ds(off, step), :] = val

    scopies = [ship(0, 3, 0, 1), ship(1, 3, 1, 2), ship(2, 1, 0, 1), ship(3, 2, 1, 2)]
    partial(0, 0, keep)
    c1.wait_recv()
    cnts[4] = cnts[2] + cnts[3]
    c2 = remote(cnts.at[4], cnts.at[5], cs.at[2], cr.at[2], same(2))
    scopies[1].wait_recv()
    scopies.append(ship(4, 1, 1, 1, add=1))
    scopies[0].wait_recv()
    scopies.append(ship(5, 2, 0, 2, add=0))
    partial(0, 1, keep)

    lw.wait()
    for rel in (0, 1, 2, 3):
        for c in ((), (wx1,), (wy0,), (fy0, fx1))[rel]:
            c.wait_recv()
        cols = pl.ds(pl.multiple_of(same(rel) * R, R), R)
        a = jnp.dot(x[:, cols], wg[rel], preferred_element_type=F32)
        b = jnp.dot(xp[rel], wg[rel], preferred_element_type=F32)
        if rel == 0:
            vown[...] = a
            vsend[...] = b
        else:
            vown[...] += a
            vsend[...] += b
    vcopy = remote(vsend, vrecv, vs, vr, peer)
    vcopy.wait_recv()
    vown[...] += vrecv[...]

    def contexts(kh, _):
        kcols = pl.ds(pl.multiple_of(kh * HEAD_SIZE, HEAD_SIZE), HEAD_SIZE)
        val = vown[:, kcols].astype(BF16)
        for h in range(GROUP):
            cols = pl.ds(pl.multiple_of((kh * GROUP + h) * HEAD_SIZE, HEAD_SIZE), HEAD_SIZE)
            ctx[:, cols] = dot_tt(pt[kh * GROUP + h], val).astype(BF16)
        return 0

    lax.fori_loop(0, kv, contexts, 0)

    c2.wait_recv()
    inv = 1.0 / (cnts[4] + cnts[5])[0:1, 0:1]
    for part in (0, 1):
        scopies[2 + part].wait_recv()
        acc[half[part], :] += recvbuf[2 + part].astype(F32)
    for part in (1, 0):
        scopies[5 - part].wait_recv()
        dw_ref[half[part], :] = (acc[half[part], :] + recvbuf[5 - part].astype(F32)) * inv
    for c in [wx0, wx1, wy0, wy1, fx1, fy0, dcopy, vcopy, c0, c1, c2] + xcopies + scopies:
        c.wait_send()


def write_kernel(ctx, dw, ctx_hbm, dw_hbm, sems):
    copies = []
    for src, dst in ((ctx, ctx_hbm), (dw, dw_hbm)):
        rows = src.shape[0] // 2
        for part in range(2):
            here = pl.ds(part * rows, rows)
            copies.append(
                pltpu.make_async_copy(src.at[here], dst.at[here], sems.at[len(copies)])
            )
    for c in copies:
        c.start()
    for c in copies:
        c.wait()


def fused(hidden_in, queries, keys, value_weight, context_grad, doc_ids, token_counts):
    T, M = hidden_in.shape
    C = keys.shape[1]
    Q = queries.shape[1]
    R = value_weight.shape[0]
    heads = Q // HEAD_SIZE
    hbm = pl.BlockSpec(memory_space=pltpu.HBM)
    dma = pltpu.SemaphoreType.DMA
    pinned = [
        pltpu.with_memory_space_constraint(a, pltpu.HBM)
        for a in (hidden_in, queries, keys, value_weight, context_grad, doc_ids)
    ]
    results = tuple(
        pl.pallas_call(
            fused_kernel,
            out_shape=(
                jax.ShapeDtypeStruct((T, Q), BF16),
                jax.ShapeDtypeStruct((R, C), F32),
            ),
            in_specs=[hbm] * 6 + [pl.BlockSpec(memory_space=pltpu.SMEM)],
            out_specs=(pl.BlockSpec(memory_space=pltpu.VMEM),) * 2,
            scratch_shapes=[
                pltpu.VMEM((T, M), BF16),
                pltpu.VMEM((4, T, R), BF16),
                pltpu.VMEM((T, Q), BF16),
                pltpu.VMEM((T, C), BF16),
                pltpu.VMEM((T, Q), BF16),
                pltpu.VMEM((4, R, C), BF16),
                pltpu.VMEM((heads, T, T), BF16),
                pltpu.VMEM((T, T), F32),
                pltpu.VMEM((T, C), BF16),
                pltpu.VMEM((T, C), BF16),
                pltpu.VMEM((T, C), F32),
                pltpu.VMEM((T, C), F32),
                pltpu.VMEM((T, C), F32),
                pltpu.VMEM((6, R // 2, C), BF16),
                pltpu.VMEM((6, R // 2, C), BF16),
                pltpu.VMEM((R, C), F32),
                pltpu.VMEM((6, 8, 128), F32),
                pltpu.VMEM(doc_ids.shape, jnp.int32),
                dma((6,)),
                dma((4,)), dma((4,)),
                dma((6,)), dma((6,)),
                dma((3,)), dma((3,)),
                dma, dma, dma, dma,
                dma((6,)), dma((6,)),
            ],
            compiler_params=pltpu.CompilerParams(
                collective_id=0, has_side_effects=True, vmem_limit_bytes=48 * 1024 * 1024
            ),
        )(*pinned, token_counts)
    )
    return tuple(
        pl.pallas_call(
            write_kernel,
            out_shape=tuple(jax.ShapeDtypeStruct(a.shape, a.dtype) for a in results),
            in_specs=[pl.BlockSpec(memory_space=pltpu.VMEM)] * 2,
            out_specs=(hbm, hbm),
            scratch_shapes=[dma((4,))],
        )(*(pltpu.with_memory_space_constraint(a, pltpu.VMEM) for a in results))
    )


def solution(mesh):
    in_specs = (
        P("dp", None),
        P("dp", "tensor"),
        P("dp", "tensor"),
        P("dp", "tensor"),
        P("dp", "tensor"),
        P("dp", None),
        P("dp"),
    )
    out_specs = (P("dp", "tensor"), P("dp", "tensor"))
    body = fused if mesh.shape["dp"] == 8 else plain
    return jax.shard_map(body, mesh=mesh, in_specs=in_specs, out_specs=out_specs, check_vma=False)
```
